768 devices in a mesh: section: 48 (over y_lo, z, core), tensor: 4 (over y_hi), dp: 4 (over x).
Axes of the slice: x: 4, y: 8 (y_hi: 4, y_lo: 2; y = y_hi * 2 + y_lo), z: 12, core: 2. Of those that a mesh axis runs over, the one named last changes fastest.
Arguments:
- hidden: bfloat16 [1536, 8192], P(('section', 'dp'), 'tensor'), may hold values from -250 to 250
- vocab_weight: bfloat16 [8192, 122880], P(None, ('section', 'tensor')), may hold values from -0.6 to 0.6
- target_ids: int32 [1536], P(('section', 'dp')), may hold values from 0 to 122879
- ref_logp: float32 [1536], P(('section', 'dp')), may hold values from -8 to -0.5
- response_lengths: int32 [192], P(('section', 'dp')), may hold values from 1 to 8
Outputs:
- token_logp: float32 [1536], P(('section', 'dp'))
- entropy: float32 [1536], P(('section', 'dp'))
- kl_term: float32 [1536], P(('section', 'dp'))
The draws below stay inside these ranges and needn't reach their ends.
All inputs are finite; a program needn't handle non-finite values.
Results may differ from the reference program's by a relative error of at most 0.0015.
Values may be sent and summed in bfloat16 or wider, within the bound.
No kernel may reach another device: no remote copies, remote signals or barrier semaphores. Data moves between devices by JAX's collectives and lax.ppermute only.
A program may use at most 64 MiB of HBM per device.

```python
import math
import jax
import jax.numpy as jnp
import numpy as np
from jax import lax

D = 8192
VOC_DEV = 640
VOCAB = 122880
TOKENS = 1536
SPAN = 8
SEQS = 192


def feature_mean(key):
    return jnp.clip(0.1 * jax.random.normal(jax.random.fold_in(key, 99), (D,), jnp.float32), -0.4, 0.4)


def draw_vocab_weight(key, part):
    noise = jnp.clip(0.033 * jax.random.normal(jax.random.fold_in(key, 31), (D, VOCAB), jnp.float32), -0.2, 0.2)
    return (noise + feature_mean(key)[:, None]).astype(jnp.bfloat16)


def draw_hidden(key, part):
    first = jax.random.fold_in(jax.random.fold_in(key, 17), 0)
    values = jax.random.normal(first, (TOKENS, D), jnp.float32)
    values = jnp.clip(values, -6.0, 6.0)
    mean = feature_mean(key)
    direction = mean / jnp.sum(mean * mean)
    chosen = jax.random.bernoulli(jax.random.fold_in(key, 41), 0.25, (TOKENS, 1)).astype(jnp.float32)
    shift = jax.random.uniform(jax.random.fold_in(key, 43), (TOKENS, 1), jnp.float32, 220.0, 450.0)
    values = jnp.clip(values + chosen * shift * direction[None, :], -250.0, 250.0)
    return values.astype(jnp.bfloat16)


def touch_ends(entries, own_key, low, largest):
    shape = entries.shape
    index_at = [jax.random.randint(jax.random.fold_in(own_key, axis), (), 0, shape[axis]) for axis in range(len(shape))]
    entries = entries.at[tuple(index_at)].set(low)
    longest = shape.index(max(shape))
    index_at[longest] = (index_at[longest] + 1) % shape[longest]
    return entries.at[tuple(index_at)].set(largest)


def level_of(own_key, shape, pieces, smallest, top_value):
    def one(axis_at, parts):
        steps = jax.random.uniform(jax.random.fold_in(jax.random.fold_in(own_key, 6), axis_at), (parts,), jnp.float32, smallest / len(pieces), top_value / len(pieces))
        return jnp.repeat(jnp.exp(steps), shape[axis_at] // parts).reshape((-1,) + (1,) * (len(shape) - axis_at - 1))

    gain = one(*pieces[0])
    for cut in pieces[1:]:
        gain = gain * one(*cut)
    return gain


def skewed_wide(own_key, dims, amount, skew):
    loads = [min(1 << octave, amount + 1 - (1 << octave)) * (1 << 20) // math.isqrt((1 << octave) ** skew) + 1 for octave in range((amount + 1).bit_length()) if 1 << octave <= amount]
    deviation = 1 + sum(loads) // (1 << 30)
    listing = np.cumsum(np.array([max(1, weight // deviation) for weight in loads]))
    lot = jax.random.randint(jax.random.fold_in(own_key, 1), dims, 0, int(listing[len(loads) - 1]))
    start = jnp.left_shift(1, jnp.searchsorted(jnp.asarray(listing, jnp.int32), lot, side="right").astype(jnp.int32))
    grade = start - 1 + jax.random.randint(jax.random.fold_in(own_key, 4), dims, 0, 1 << 30) % jnp.minimum(start, amount + 1 - start)
    return jax.random.permutation(jax.random.fold_in(own_key, 2), amount)[grade].astype(jnp.int32)


def setup_inputs(seed: int = 0) -> dict:
    key_list = jax.random.split(jax.random.key(seed), 6)
    return {
        "hidden": draw_hidden(jax.random.fold_in(key_list[5], 71), 0),
        "vocab_weight": draw_vocab_weight(jax.random.fold_in(key_list[5], 71), 0),
        "target_ids": touch_ends(skewed_wide(key_list[2], (TOKENS,), VOCAB, 2), jax.random.fold_in(key_list[2], 3), 0, VOCAB - 1).astype(jnp.int32),
        "ref_logp": jnp.clip(-8.0 + 7.5 * jax.random.uniform(key_list[3], (TOKENS,), jnp.float32) ** level_of(key_list[3], (TOKENS,), ((0, 192),), -0.2, 0.2), -8.0, -0.5),
        "response_lengths": touch_ends(jax.random.randint(key_list[4], (SEQS,), 1, SPAN + 1), jax.random.fold_in(key_list[4], 1), 1, SPAN).astype(jnp.int32),
    }


def block_stats(hidden_f, vocab_weight, target_ids, index):
    start = index * VOC_DEV
    cols = lax.dynamic_slice_in_dim(vocab_weight, start, VOC_DEV, 1).astype(jnp.float32)
    logits = jnp.dot(hidden_f, cols, preferred_element_type=jnp.float32)
    top = jnp.max(logits, axis=1)
    expo = jnp.exp(logits - top[:, None])
    total = jnp.sum(expo, axis=1)
    moment = jnp.sum(expo * logits, axis=1)
    column = start + jnp.arange(VOC_DEV, dtype=jnp.int32)
    picked = jnp.sum(jnp.where(target_ids[:, None] == column[None, :], logits, 0.0), axis=1)
    return top, total, moment, picked


def reference(hidden, vocab_weight, target_ids, ref_logp, response_lengths):
    hidden_f = hidden.astype(jnp.float32)
    count = VOCAB // VOC_DEV
    tops, totals, moments, pickeds = lax.map(lambda k: block_stats(hidden_f, vocab_weight, target_ids, k), jnp.arange(count, dtype=jnp.int32))
    top = jnp.max(tops, axis=0)
    scale = jnp.exp(tops - top[None, :])
    total = jnp.sum(totals * scale, axis=0)
    moment = jnp.sum(moments * scale, axis=0)
    picked = jnp.sum(pickeds, axis=0)
    lse = top + jnp.log(total)
    logp = picked - lse
    ent = lse - moment / total
    token = jnp.arange(TOKENS, dtype=jnp.int32)
    owner = token // SPAN
    slot = token % SPAN
    live = (slot < response_lengths[owner]).astype(jnp.float32)
    return logp * live, ent * live, (logp - ref_logp) * live
```

```python
import jax
import jax.numpy as jnp
from jax import lax
from jax.sharding import PartitionSpec as P

NY, NZ = 8, 12
PLANE = ("section", "tensor")
LANES = 128

Z_OFF = ((0, 6, 3, 9), (0, 6, 9, 3))
SPREAD = (0, 1, 11)


def place(y, z, core):
    y, z = y % NY, z % NZ
    return ((y % 2) * NZ * 2 + z * 2 + core) * (NY // 2) + y // 2


def fetch(x, shifts):
    pairs = [
        (place(y + shifts[c][0], z + shifts[c][1], c ^ shifts[c][2]), place(y, z, c))
        for y in range(NY)
        for z in range(NZ)
        for c in range(2)
    ]
    return lax.ppermute(x, PLANE, pairs)


def same(dy, dz, dc=0):
    return ((dy, dz, dc), (dy, dz, dc))


def z_rank():
    table = []
    for c in range(2):
        held = [(off + e) % NZ for e in SPREAD for off in Z_OFF[c]]
        table.append([held.index(d) for d in range(NZ)])
    return table


def gather_rows(hidden, target_ids, core, y_hi):
    row_dev, feat = hidden.shape
    digits = jnp.stack([target_ids % 256, (target_ids // 256) % 256, target_ids // 65536], axis=1)
    digits = jnp.pad(digits.astype(jnp.bfloat16), ((0, 0), (0, LANES - 3)))
    x = jnp.concatenate([hidden, digits], axis=1)[None]
    x = jnp.concatenate([x, fetch(x, same(0, 6))], axis=0)
    x = x[None]
    x = jnp.concatenate([x, fetch(x, same(4, 0))], axis=0)
    x = jnp.concatenate([x, fetch(x, ((0, 3, 0), (0, -3, 0)))], axis=1)
    x = jnp.concatenate([x, fetch(x, ((2, 0, 0), (-2, 0, 0)))], axis=0)
    x = x.reshape(4, 4 * row_dev, feat + LANES)
    rel = [jnp.mod(j - y_hi, 4) for j in range(4)]
    slot = [
        jnp.where(r == 0, 0, jnp.where(r == 2, 1, jnp.where((r == 1) == (core == 0), 2, 3)))
        for r in rel
    ]
    pieces = [lax.dynamic_index_in_dim(x, s, 0, False)[:, :feat] for s in slot]
    x = jnp.concatenate(pieces + [x[0][:, feat:]], axis=1)
    x = jnp.concatenate([x, fetch(x, same(0, 1)), fetch(x, same(0, -1))], axis=0)
    half = x.shape[0] // 2
    x = jnp.concatenate([x, fetch(x[:half], same(1, 0)), fetch(x[half:], same(-1, 0))], axis=0)
    return jnp.concatenate([x, fetch(x, same(0, 0, 1))], axis=0)


def per_device(hidden, vocab_weight, target_ids, ref_logp, response_lengths):
    row_dev = hidden.shape[0]
    depth, voc_dev = vocab_weight.shape
    section, y_hi = lax.axis_index("section"), lax.axis_index("tensor")
    core, z, y_lo = section % 2, (section // 2) % NZ, section // (2 * NZ)
    n_sec, n_ten = 4 * NZ, NY // 2

    rows = gather_rows(hidden, target_ids, core, y_hi)
    digits = rows[:, depth : depth + 3].astype(jnp.int32)
    ids = (digits[:, 2] * 256 + digits[:, 1]) * 256 + digits[:, 0]
    logits = jnp.dot(rows[:, :depth], vocab_weight, preferred_element_type=jnp.float32)
    top = jnp.max(logits, axis=1)
    expo = jnp.exp(logits - top[:, None])
    total = jnp.sum(expo, axis=1)
    moment = jnp.sum(expo * logits, axis=1)
    column = (section * n_ten + y_hi) * voc_dev + jnp.arange(voc_dev, dtype=jnp.int32)
    picked = jnp.sum(jnp.where(ids[:, None] == column[None, :], logits, 0.0), axis=1)

    s = jnp.arange(n_sec, dtype=jnp.int32)
    s_core, s_z, s_y = s % 2, (s // 2) % NZ, s // (2 * NZ)
    ranks = jnp.asarray(z_rank(), jnp.int32)
    away = jnp.mod(s_z - z, NZ)
    flat = ranks.reshape(-1)
    pick = (s_core * NZ + away)[:, None] == jnp.arange(2 * NZ, dtype=jnp.int32)[None, :]
    rank = jnp.sum(jnp.where(pick, flat[None, :], 0), axis=1)
    group = jnp.where(s_core == core, 0, 2 * NZ) + jnp.where(s_y == y_lo, 0, NZ) + rank
    stats = jnp.stack([top, total, moment, picked], axis=0).reshape(4, n_sec, row_dev)
    stats = stats.transpose(1, 0, 2).reshape(n_sec, 4 * row_dev)
    choose = (group[:, None] == s[None, :]).astype(jnp.float32)
    stats = jnp.dot(choose, stats, precision=lax.Precision.HIGHEST)
    send = jnp.broadcast_to(
        stats.reshape(n_sec, 1, 4, row_dev), (n_sec, n_ten, 4, row_dev)
    ).reshape(n_sec * n_ten, 4, row_dev)
    got = lax.all_to_all(send, PLANE, 0, 0)

    tops = got[:, 0]
    top = jnp.max(tops, axis=0)
    scale = jnp.exp(tops - top[None])
    total = jnp.sum(got[:, 1] * scale, axis=0)
    moment = jnp.sum(got[:, 2] * scale, axis=0)
    picked = jnp.sum(got[:, 3], axis=0)
    lse = top + jnp.log(total)
    logp = picked - lse
    ent = lse - moment / total
    slot = jnp.arange(row_dev, dtype=jnp.int32)
    live = (slot < response_lengths[0]).astype(jnp.float32)
    return (logp * live, ent * live, (logp - ref_logp) * live)


def solution(mesh):
    in_specs = (
        P(("section", "dp"), "tensor"),
        P(None, ("section", "tensor")),
        P(("section", "dp")),
        P(("section", "dp")),
        P(("section", "dp")),
    )
    out_specs = (P(("section", "dp")), P(("section", "dp")), P(("section", "dp")))
    return jax.shard_map(
        per_device, mesh=mesh, in_specs=in_specs, out_specs=out_specs, check_vma=False
    )
```

```python
import functools

import jax
import jax.numpy as jnp
from jax import lax
from jax.experimental import pallas as pl
from jax.experimental.pallas import tpu as pltpu
from jax.sharding import Mesh, PartitionSpec as P

NY, NZ, NR = 8, 12, 3
NQ = NZ // NR
LANES = 128
CHUNK = 1024
PLANE = ("y_lo", "zq", "zr", "core", "tensor")

GROUP = (((0, 12, 24), (8, 28, 32)), ((4, 20, 36), (16, 40, 44)))


def place(y, z, core):
    y, z = y % NY, z % NZ
    return ((y % 2) * NZ * 2 + z * 2 + core) * (NY // 2) + y // 2


def fetch(x, dy, dz, dcore=0):
    pairs = [
        (place(y + dy, z + dz, c ^ dcore), place(y, z, c))
        for y in range(NY)
        for z in range(NZ)
        for c in range(2)
    ]
    return lax.ppermute(x, PLANE, pairs)


def stats_kernel(pieces, chunk, offset_ref, *refs):
    rows, (w_ref, out_ref, acc) = refs[:pieces], refs[pieces:]
    depth = w_ref.shape[0]
    for k in range(depth // chunk):
        x = jnp.concatenate([r[:, k * chunk : (k + 1) * chunk] for r in rows], axis=0)
        part = jnp.dot(x, w_ref[k * chunk : (k + 1) * chunk, :], preferred_element_type=jnp.float32)
        if k == 0:
            acc[...] = part
        else:
            acc[...] += part
    logits = acc[...]
    digits = jnp.concatenate([r[:, depth:] for r in rows], axis=0).astype(jnp.float32)
    ids = (digits[:, 2:3] * 256 + digits[:, 1:2]) * 256 + digits[:, 0:1]
    column = lax.broadcasted_iota(jnp.int32, logits.shape, 1) + offset_ref[0]
    top = jnp.max(logits, axis=1, keepdims=True)
    expo = jnp.exp(logits - top)
    total = jnp.sum(expo, axis=1, keepdims=True)
    moment = jnp.sum(expo * logits, axis=1, keepdims=True)
    hit = column == ids.astype(jnp.int32)
    picked = jnp.sum(jnp.where(hit, logits, 0.0), axis=1, keepdims=True)
    lane = lax.broadcasted_iota(jnp.int32, out_ref.shape, 1)
    low = jnp.where(lane == 0, top, total)
    high = jnp.where(lane == 2, moment, picked)
    out_ref[...] = jnp.where(lane < 2, low, high)


def stats_of(rows, weight, offset):
    count = sum(r.shape[0] for r in rows)
    depth, voc_dev = weight.shape
    return pl.pallas_call(
        functools.partial(stats_kernel, len(rows), CHUNK),
        out_shape=jax.ShapeDtypeStruct((count, LANES), jnp.float32),
        in_specs=[pl.BlockSpec(memory_space=pltpu.SMEM)]
        + [pl.BlockSpec(memory_space=pltpu.VMEM)] * (len(rows) + 1),
        out_specs=pl.BlockSpec(memory_space=pltpu.VMEM),
        scratch_shapes=[
            pltpu.VMEM((count, voc_dev), jnp.float32),
        ],
        compiler_params=pltpu.CompilerParams(vmem_limit_bytes=16 * 2**20),
        cost_estimate=pl.CostEstimate(
            flops=2 * count * depth * voc_dev,
            bytes_accessed=2 * depth * (count + voc_dev),
            transcendentals=count * voc_dev,
        ),
    )(offset, *rows, weight)


def per_device(hidden, vocab_weight, target_ids, ref_logp, response_lengths):
    row_dev, feat = hidden.shape
    voc_dev = vocab_weight.shape[1]
    y_lo, y_hi = lax.axis_index("y_lo"), lax.axis_index("tensor")
    core = lax.axis_index("core")
    z = lax.axis_index("zq") * NR + lax.axis_index("zr")
    section = (y_lo * NZ + z) * 2 + core
    n_sec, n_ten = 4 * NZ, NY // 2
    offset = ((section * n_ten + y_hi) * voc_dev).reshape(1).astype(jnp.int32)

    digits = jnp.stack([target_ids % 256, (target_ids // 256) % 256, target_ids // 65536], axis=1)
    digits = jnp.pad(digits.astype(jnp.bfloat16), ((0, 0), (0, LANES - 3)))
    block = jnp.concatenate([hidden, digits], axis=1)
    block = jnp.broadcast_to(block[None], (NQ * n_ten,) + block.shape)
    block = lax.all_to_all(block, ("zq", "tensor"), 0, 0)
    block = block.reshape(NQ, n_ten, row_dev, feat + LANES)
    pieces = [block[:, h, :, :feat] for h in range(n_ten)] + [block[:, 0, :, feat:]]
    unit = NQ * row_dev
    near = jnp.concatenate(pieces, axis=2).reshape(unit, n_ten * feat + LANES)

    near_p = fetch(near, 0, 0, 1)
    hops = []
    for dy, dz in ((1, 0), (0, 1), (0, -1), (-1, 1), (-1, -1)):
        hops.append(fetch(near, dy, dz))
    stats_a = stats_of([near, near_p], vocab_weight, offset)
    early = jnp.concatenate(hops[:2], axis=0)
    early_p = fetch(early, 0, 0, 1)
    late = jnp.concatenate(hops[2:], axis=0)
    late_p = fetch(late, 0, 0, 1)
    stats_b = stats_of([early, early_p, late], vocab_weight, offset)
    stats_c = stats_of([late_p], vocab_weight, offset)

    s = jnp.arange(n_sec, dtype=jnp.int32)
    s_core, s_z, s_y = s % 2, (s // 2) % NZ, s // (2 * NZ)
    entry = jnp.where(s_core == core, 0, 2 * NR) + ((s_y + y_lo) % 2) * NR + (s_z - z) % NR
    table = [first for c in GROUP for row in c for first in row]
    group = sum(jnp.where(entry == i, first, 0) for i, first in enumerate(table)) + s_z // NR
    stats = jnp.concatenate([stats_a[:, :4], stats_b[:, :4], stats_c[:, :4]], axis=0)
    stats = stats.reshape(n_sec, 4 * row_dev)
    choose = (group[:, None] == s[None, :]).astype(jnp.float32)
    stats = jnp.dot(choose, stats, precision=lax.Precision.HIGHEST)
    send = jnp.broadcast_to(stats[:, None, :], (n_sec, n_ten, 4 * row_dev))
    send = send.reshape(n_sec * n_ten, 1, 4 * row_dev)
    got = lax.all_to_all(send, PLANE, 0, 0).reshape(n_sec * n_ten, row_dev, 4)

    tops = got[:, :, 0]
    top = jnp.max(tops, axis=0)
    scale = jnp.exp(tops - top[None])
    total = jnp.sum(got[:, :, 1] * scale, axis=0)
    moment = jnp.sum(got[:, :, 2] * scale, axis=0)
    picked = jnp.sum(got[:, :, 3], axis=0)
    lse = top + jnp.log(total)
    logp = picked - lse
    ent = lse - moment / total
    slot = jnp.arange(row_dev, dtype=jnp.int32)
    live = (slot < response_lengths[0]).astype(jnp.float32)
    return (logp * live, ent * live, (logp - ref_logp) * live)


def solution(mesh):
    tensor, dp = mesh.shape["tensor"], mesh.shape["dp"]
    mesh = Mesh(
        mesh.devices.reshape(2, NQ, NR, 2, tensor, dp), ("y_lo", "zq", "zr", "core", "tensor", "dp")
    )
    section = ("y_lo", "zq", "zr", "core")
    rows = P(section + ("dp",))
    in_specs = (P(section + ("dp",), "tensor"), P(None, section + ("tensor",)), rows, rows, rows)
    return jax.shard_map(
        per_device, mesh=mesh, in_specs=in_specs, out_specs=(rows, rows, rows), check_vma=False
    )
```

```python
import functools

import jax
import jax.numpy as jnp
from jax import lax
from jax.experimental import pallas as pl
from jax.experimental.pallas import tpu as pltpu
from jax.sharding import Mesh, PartitionSpec as P

NY, NZ, NR = 8, 12, 3
NQ = NZ // NR
LANES = 128
CHUNK = 1024
PLANE = ("y_lo", "zq", "zr", "core", "tensor")


def place(y, z, core):
    y, z = y % NY, z % NZ
    return ((y % 2) * NZ * 2 + z * 2 + core) * (NY // 2) + y // 2


def fetch(x, dz=0, across=False, swap=False):
    pairs = [
        (place(y + (1 - 2 * c if across else 0), z + dz, c ^ swap), place(y, z, c))
        for y in range(NY)
        for z in range(NZ)
        for c in range(2)
    ]
    return lax.ppermute(x, PLANE, pairs)


def stats_kernel(pieces, chunk, offset_ref, *refs):
    rows, (w_ref, out_ref, acc) = refs[:pieces], refs[pieces:]
    depth = w_ref.shape[0]
    for k in range(depth // chunk):
        x = jnp.concatenate([r[:, k * chunk : (k + 1) * chunk] for r in rows], axis=0)
        part = jnp.dot(x, w_ref[k * chunk : (k + 1) * chunk, :], preferred_element_type=jnp.float32)
        if k == 0:
            acc[...] = part
        else:
            acc[...] += part
    logits = acc[...]
    digits = jnp.concatenate([r[:, depth:] for r in rows], axis=0).astype(jnp.float32)
    ids = (digits[:, 2:3] * 256 + digits[:, 1:2]) * 256 + digits[:, 0:1]
    column = lax.broadcasted_iota(jnp.int32, logits.shape, 1) + offset_ref[0]
    top = jnp.max(logits, axis=1, keepdims=True)
    expo = jnp.exp(logits - top)
    total = jnp.sum(expo, axis=1, keepdims=True)
    moment = jnp.sum(expo * logits, axis=1, keepdims=True)
    hit = column == ids.astype(jnp.int32)
    picked = jnp.sum(jnp.where(hit, logits, 0.0), axis=1, keepdims=True)
    lane = lax.broadcasted_iota(jnp.int32, out_ref.shape, 1)
    low = jnp.where(lane == 0, top, total)
    high = jnp.where(lane == 2, moment, picked)
    out_ref[...] = jnp.where(lane < 2, low, high)


def stats_of(rows, weight, offset):
    count = sum(r.shape[0] for r in rows)
    depth, voc_dev = weight.shape
    return pl.pallas_call(
        functools.partial(stats_kernel, len(rows), CHUNK),
        out_shape=jax.ShapeDtypeStruct((count, LANES), jnp.float32),
        in_specs=[pl.BlockSpec(memory_space=pltpu.SMEM)]
        + [pl.BlockSpec(memory_space=pltpu.VMEM)] * (len(rows) + 1),
        out_specs=pl.BlockSpec(memory_space=pltpu.VMEM),
        scratch_shapes=[
            pltpu.VMEM((count, voc_dev), jnp.float32),
        ],
        compiler_params=pltpu.CompilerParams(vmem_limit_bytes=16 * 2**20),
        cost_estimate=pl.CostEstimate(
            flops=2 * count * depth * voc_dev,
            bytes_accessed=2 * depth * (count + voc_dev),
            transcendentals=count * voc_dev,
        ),
    )(offset, *rows, weight)


def per_device(hidden, vocab_weight, target_ids, ref_logp, response_lengths):
    row_dev, feat = hidden.shape
    voc_dev = vocab_weight.shape[1]
    y_lo, y_hi = lax.axis_index("y_lo"), lax.axis_index("tensor")
    core = lax.axis_index("core")
    z = lax.axis_index("zq") * NR + lax.axis_index("zr")
    section = (y_lo * NZ + z) * 2 + core
    n_sec, n_ten = 4 * NZ, NY // 2
    offset = ((section * n_ten + y_hi) * voc_dev).reshape(1).astype(jnp.int32)

    digits = jnp.stack([target_ids % 256, (target_ids // 256) % 256, target_ids // 65536], axis=1)
    digits = jnp.pad(digits.astype(jnp.bfloat16), ((0, 0), (0, LANES - 3)))
    block = jnp.concatenate([hidden, digits], axis=1)
    block = jnp.broadcast_to(block[None], (NQ * n_ten,) + block.shape)
    block = lax.all_to_all(block, ("zq", "tensor"), 0, 0)
    block = block.reshape(NQ, n_ten, row_dev, feat + LANES)
    pieces = [block[:, h, :, :feat] for h in range(n_ten)] + [block[:, 0, :, feat:]]
    unit = NQ * row_dev
    near = jnp.concatenate(pieces, axis=2).reshape(unit, n_ten * feat + LANES)

    up = fetch(near, dz=1)
    down = fetch(near, dz=-1)
    side = fetch(near, across=True)
    side_up = fetch(up, across=True)
    side_down = fetch(down, across=True)
    early = jnp.concatenate([near, up, down], axis=0)
    early_p = fetch(early, swap=True)
    stats_a = stats_of([early], vocab_weight, offset)
    late = jnp.concatenate([side, side_up, side_down], axis=0)
    late_p = fetch(late, swap=True)
    stats_b = stats_of([early_p, late], vocab_weight, offset)
    stats_c = stats_of([late_p], vocab_weight, offset)

    s = jnp.arange(n_sec, dtype=jnp.int32)
    s_core, s_z, s_y = s % 2, (s // 2) % NZ, s // (2 * NZ)
    group = ((s_y + y_lo) % 2) * (n_sec // 2) + jnp.where(s_core == core, 0, n_sec // 4)
    group = group + ((s_z - z) % NR) * NQ + s_z // NR
    stats = jnp.concatenate([stats_a[:, :4], stats_b[:, :4], stats_c[:, :4]], axis=0)
    stats = stats.reshape(n_sec, 4 * row_dev)
    choose = (group[:, None] == s[None, :]).astype(jnp.float32)
    stats = jnp.dot(choose, stats, precision=lax.Precision.HIGHEST)
    send = jnp.broadcast_to(stats[:, None, :], (n_sec, n_ten, 4 * row_dev))
    send = send.reshape(n_sec * n_ten, 1, 4 * row_dev)
    got = lax.all_to_all(send, PLANE, 0, 0).reshape(n_sec * n_ten, row_dev, 4)

    tops = got[:, :, 0]
    top = jnp.max(tops, axis=0)
    scale = jnp.exp(tops - top[None])
    total = jnp.sum(got[:, :, 1] * scale, axis=0)
    moment = jnp.sum(got[:, :, 2] * scale, axis=0)
    picked = jnp.sum(got[:, :, 3], axis=0)
    lse = top + jnp.log(total)
    logp = picked - lse
    ent = lse - moment / total
    slot = jnp.arange(row_dev, dtype=jnp.int32)
    live = (slot < response_lengths[0]).astype(jnp.float32)
    return (logp * live, ent * live, (logp - ref_logp) * live)


def solution(mesh):
    tensor, dp = mesh.shape["tensor"], mesh.shape["dp"]
    mesh = Mesh(
        mesh.devices.reshape(2, NQ, NR, 2, tensor, dp), ("y_lo", "zq", "zr", "core", "tensor", "dp")
    )
    section = ("y_lo", "zq", "zr", "core")
    rows = P(section + ("dp",))
    in_specs = (P(section + ("dp",), "tensor"), P(None, section + ("tensor",)), rows, rows, rows)
    return jax.shard_map(
        per_device, mesh=mesh, in_specs=in_specs, out_specs=(rows, rows, rows), check_vma=False
    )
```

```python
import functools

import jax
import jax.numpy as jnp
from jax import lax
from jax.experimental import pallas as pl
from jax.experimental.pallas import tpu as pltpu
from jax.sharding import Mesh, PartitionSpec as P

NY, NZ, NR = 8, 12, 3
NQ = NZ // NR
LANES = 128
CHUNK = 1024
PLANE = ("y_lo", "zq", "zr", "core", "tensor")


def place(y, z, core):
    y, z = y % NY, z % NZ
    return ((y % 2) * NZ * 2 + z * 2 + core) * (NY // 2) + y // 2


def fetch(x, dz=0, across=False, swap=False):
    pairs = [
        (place(y + (1 - 2 * c if across else 0), z + dz, c ^ swap), place(y, z, c))
        for y in range(NY)
        for z in range(NZ)
        for c in range(2)
    ]
    return lax.ppermute(x, PLANE, pairs)


def stats_kernel(pieces, chunk, offset_ref, *refs):
    rows, (w_ref, out_ref, acc) = refs[:pieces], refs[pieces:]
    depth = w_ref.shape[0]
    for k in range(depth // chunk):
        x = jnp.concatenate([r[:, k * chunk : (k + 1) * chunk] for r in rows], axis=0)
        part = jnp.dot(x, w_ref[k * chunk : (k + 1) * chunk, :], preferred_element_type=jnp.float32)
        if k == 0:
            acc[...] = part
        else:
            acc[...] += part
    logits = acc[...]
    digits = jnp.concatenate([r[:, depth:] for r in rows], axis=0).astype(jnp.float32)
    ids = (digits[:, 2:3] * 256 + digits[:, 1:2]) * 256 + digits[:, 0:1]
    column = lax.broadcasted_iota(jnp.int32, logits.shape, 1) + offset_ref[0]
    top = jnp.max(logits, axis=1, keepdims=True)
    expo = jnp.exp(logits - top)
    total = jnp.sum(expo, axis=1, keepdims=True)
    moment = jnp.sum(expo * logits, axis=1, keepdims=True)
    hit = column == ids.astype(jnp.int32)
    picked = jnp.sum(jnp.where(hit, logits, 0.0), axis=1, keepdims=True)
    lane = lax.broadcasted_iota(jnp.int32, out_ref.shape, 1)
    low = jnp.where(lane == 0, top, total)
    high = jnp.where(lane == 2, moment, picked)
    out_ref[...] = jnp.where(lane < 2, low, high)


def stats_of(rows, weight, offset):
    count = sum(r.shape[0] for r in rows)
    depth, voc_dev = weight.shape
    return pl.pallas_call(
        functools.partial(stats_kernel, len(rows), CHUNK),
        out_shape=jax.ShapeDtypeStruct((count, LANES), jnp.float32),
        in_specs=[pl.BlockSpec(memory_space=pltpu.SMEM)]
        + [pl.BlockSpec(memory_space=pltpu.VMEM)] * (len(rows) + 1),
        out_specs=pl.BlockSpec(memory_space=pltpu.VMEM),
        scratch_shapes=[
            pltpu.VMEM((count, voc_dev), jnp.float32),
        ],
        compiler_params=pltpu.CompilerParams(vmem_limit_bytes=16 * 2**20),
        cost_estimate=pl.CostEstimate(
            flops=2 * count * depth * voc_dev,
            bytes_accessed=2 * depth * (count + voc_dev),
            transcendentals=count * voc_dev,
        ),
    )(offset, *rows, weight)


def per_device(hidden, vocab_weight, target_ids, ref_logp, response_lengths):
    row_dev, feat = hidden.shape
    voc_dev = vocab_weight.shape[1]
    y_lo, y_hi = lax.axis_index("y_lo"), lax.axis_index("tensor")
    core = lax.axis_index("core")
    z = lax.axis_index("zq") * NR + lax.axis_index("zr")
    section = (y_lo * NZ + z) * 2 + core
    n_sec, n_ten = 4 * NZ, NY // 2
    offset = ((section * n_ten + y_hi) * voc_dev).reshape(1).astype(jnp.int32)

    digits = jnp.stack([target_ids % 256, (target_ids // 256) % 256, target_ids // 65536], axis=1)
    digits = jnp.pad(digits.astype(jnp.bfloat16), ((0, 0), (0, LANES - 3)))
    block = jnp.concatenate([hidden, digits], axis=1)
    block = jnp.broadcast_to(block[None], (NQ * n_ten,) + block.shape)
    block = lax.all_to_all(block, ("zq", "tensor"), 0, 0)
    block = block.reshape(NQ, n_ten, row_dev, feat + LANES)
    pieces = [block[:, h, :, :feat] for h in range(n_ten)] + [block[:, 0, :, feat:]]
    unit = NQ * row_dev
    near = jnp.concatenate(pieces, axis=2).reshape(unit, n_ten * feat + LANES)

    up = fetch(near, dz=1)
    down = fetch(near, dz=-1)
    side = fetch(near, across=True)
    side_up = fetch(up, across=True)
    side_down = fetch(down, across=True)
    early = jnp.concatenate([near, up, down], axis=0)
    early_p = fetch(early, swap=True)
    stats_o = stats_of([near], vocab_weight, offset)
    stats_a = stats_of([up, down], vocab_weight, offset)
    mid = jnp.concatenate([side, side_up], axis=0)
    mid_p = fetch(mid, swap=True)
    stats_b = stats_of([early_p, mid], vocab_weight, offset)
    late_p = fetch(side_down, swap=True)
    stats_c = stats_of([mid_p, side_down, late_p], vocab_weight, offset)

    s = jnp.arange(n_sec, dtype=jnp.int32)
    s_core, s_z, s_y = s % 2, (s // 2) % NZ, s // (2 * NZ)
    theirs = (s_core != core).astype(jnp.int32)
    away = (s_z - z) % NR
    far = jnp.where(away < 2, 24 + 8 * theirs + NQ * away, 40 + 4 * theirs)
    group = jnp.where(s_y == y_lo, 12 * theirs + NQ * away, far) + s_z // NR
    stats = jnp.concatenate([x[:, :4] for x in (stats_o, stats_a, stats_b, stats_c)], axis=0)
    stats = stats.reshape(n_sec, 4 * row_dev)
    choose = (group[:, None] == s[None, :]).astype(jnp.float32)
    stats = jnp.dot(choose, stats, precision=lax.Precision.HIGHEST)
    send = jnp.broadcast_to(stats[:, None, :], (n_sec, n_ten, 4 * row_dev))
    send = send.reshape(n_sec * n_ten, 1, 4 * row_dev)
    got = lax.all_to_all(send, PLANE, 0, 0).reshape(n_sec * n_ten, row_dev, 4)

    tops = got[:, :, 0]
    top = jnp.max(tops, axis=0)
    scale = jnp.exp(tops - top[None])
    total = jnp.sum(got[:, :, 1] * scale, axis=0)
    moment = jnp.sum(got[:, :, 2] * scale, axis=0)
    picked = jnp.sum(got[:, :, 3], axis=0)
    lse = top + jnp.log(total)
    logp = picked - lse
    ent = lse - moment / total
    slot = jnp.arange(row_dev, dtype=jnp.int32)
    live = (slot < response_lengths[0]).astype(jnp.float32)
    return (logp * live, ent * live, (logp - ref_logp) * live)


def solution(mesh):
    tensor, dp = mesh.shape["tensor"], mesh.shape["dp"]
    mesh = Mesh(
        mesh.devices.reshape(2, NQ, NR, 2, tensor, dp), ("y_lo", "zq", "zr", "core", "tensor", "dp")
    )
    section = ("y_lo", "zq", "zr", "core")
    rows = P(section + ("dp",))
    in_specs = (P(section + ("dp",), "tensor"), P(None, section + ("tensor",)), rows, rows, rows)
    return jax.shard_map(
        per_device, mesh=mesh, in_specs=in_specs, out_specs=(rows, rows, rows), check_vma=False
    )
```

```python
import functools

import jax
import jax.numpy as jnp
from jax import lax
from jax.experimental import pallas as pl
from jax.experimental.pallas import tpu as pltpu
from jax.sharding import Mesh, PartitionSpec as P

NY, NZ, NR = 8, 12, 3
NQ = NZ // NR
LANES = 128
CHUNK = 1024
PLANE = ("y_lo", "zq", "zr", "core", "tensor")


def place(y, z, core):
    y, z = y % NY, z % NZ
    return ((y % 2) * NZ * 2 + z * 2 + core) * (NY // 2) + y // 2


def fetch(x, source):
    pairs = [
        (place(*source(y, z, c)), place(y, z, c))
        for y in range(NY)
        for z in range(NZ)
        for c in range(2)
    ]
    return lax.ppermute(x, PLANE, pairs)


def above(y, z, c):
    return y, z + 1, c


def below(y, z, c):
    return y, z - 1, c


def across(y, z, c):
    return y + 1 - 2 * c, z, c


def partner(y, z, c):
    return y, z, 1 - c


def stats_kernel(pieces, chunk, offset_ref, *refs):
    rows, (w_ref, out_ref, acc) = refs[:pieces], refs[pieces:]
    depth = w_ref.shape[0]
    for k in range(depth // chunk):
        x = jnp.concatenate([r[:, k * chunk : (k + 1) * chunk] for r in rows], axis=0)
        part = jnp.dot(x, w_ref[k * chunk : (k + 1) * chunk, :], preferred_element_type=jnp.float32)
        if k == 0:
            acc[...] = part
        else:
            acc[...] += part
    logits = acc[...]
    digits = jnp.concatenate([r[:, depth:] for r in rows], axis=0).astype(jnp.float32)
    ids = (digits[:, 2:3] * 256 + digits[:, 1:2]) * 256 + digits[:, 0:1]
    column = lax.broadcasted_iota(jnp.int32, logits.shape, 1) + offset_ref[0]
    top = jnp.max(logits, axis=1, keepdims=True)
    expo = jnp.exp(logits - top)
    total = jnp.sum(expo, axis=1, keepdims=True)
    moment = jnp.sum(expo * logits, axis=1, keepdims=True)
    hit = column == ids.astype(jnp.int32)
    picked = jnp.sum(jnp.where(hit, logits, 0.0), axis=1, keepdims=True)
    lane = lax.broadcasted_iota(jnp.int32, out_ref.shape, 1)
    low = jnp.where(lane == 0, top, total)
    high = jnp.where(lane == 2, moment, picked)
    out_ref[...] = jnp.where(lane < 2, low, high)


def stats_of(rows, weight, offset):
    count = sum(r.shape[0] for r in rows)
    depth, voc_dev = weight.shape
    return pl.pallas_call(
        functools.partial(stats_kernel, len(rows), CHUNK),
        out_shape=jax.ShapeDtypeStruct((count, LANES), jnp.float32),
        in_specs=[pl.BlockSpec(memory_space=pltpu.SMEM)]
        + [pl.BlockSpec(memory_space=pltpu.VMEM)] * (len(rows) + 1),
        out_specs=pl.BlockSpec(memory_space=pltpu.VMEM),
        scratch_shapes=[
            pltpu.VMEM((count, voc_dev), jnp.float32),
        ],
        compiler_params=pltpu.CompilerParams(vmem_limit_bytes=16 * 2**20),
        cost_estimate=pl.CostEstimate(
            flops=2 * count * depth * voc_dev,
            bytes_accessed=2 * depth * (count + voc_dev),
            transcendentals=count * voc_dev,
        ),
    )(offset, *rows, weight)


def per_device(hidden, vocab_weight, target_ids, ref_logp, response_lengths):
    row_dev, feat = hidden.shape
    voc_dev = vocab_weight.shape[1]
    y_lo, y_hi = lax.axis_index("y_lo"), lax.axis_index("tensor")
    core = lax.axis_index("core")
    z = lax.axis_index("zq") * NR + lax.axis_index("zr")
    section = (y_lo * NZ + z) * 2 + core
    n_sec, n_ten = 4 * NZ, NY // 2
    offset = ((section * n_ten + y_hi) * voc_dev).reshape(1).astype(jnp.int32)

    digits = jnp.stack([target_ids % 256, (target_ids // 256) % 256, target_ids // 65536], axis=1)
    digits = jnp.pad(digits.astype(jnp.bfloat16), ((0, 0), (0, LANES - 3)))
    block = jnp.concatenate([hidden, digits], axis=1)
    block = jnp.broadcast_to(block[None], (NQ * n_ten,) + block.shape)
    block = lax.all_to_all(block, ("zq", "tensor"), 0, 0)
    block = block.reshape(NQ, n_ten, row_dev, feat + LANES)
    pieces = [block[:, h, :, :feat] for h in range(n_ten)] + [block[:, 0, :, feat:]]
    unit = NQ * row_dev
    near = jnp.concatenate(pieces, axis=2).reshape(unit, n_ten * feat + LANES)

    up = fetch(near, above)
    down = fetch(near, below)
    side = fetch(near, across)
    side_up = jnp.where(core == 0, side, up)
    side_up = fetch(side_up, lambda y, z, c: (across if c else above)(y, z, c))
    side_down = jnp.where(core == 0, down, side)
    side_down = fetch(side_down, lambda y, z, c: (below if c else across)(y, z, c))
    early = jnp.concatenate([near, up, down, side], axis=0)
    early_p = fetch(early, partner)
    late = jnp.concatenate([side_up, side_down], axis=0)
    late_p = fetch(late, partner)
    stats_o = stats_of([near], vocab_weight, offset)
    stats_a = stats_of([up, down, side], vocab_weight, offset)
    stats_b = stats_of([early_p], vocab_weight, offset)
    stats_c = stats_of([late, late_p], vocab_weight, offset)

    s = jnp.arange(n_sec, dtype=jnp.int32)
    s_core, s_z, s_y = s % 2, (s // 2) % NZ, s // (2 * NZ)
    theirs = (s_core != core).astype(jnp.int32)
    unit = jnp.where(s_y == y_lo, 0, NR) + (s_z - z) % NR
    first = jnp.where(unit < 4, 4 * theirs + unit, 4 + 2 * theirs + unit)
    group = first * NQ + s_z // NR
    stats = jnp.concatenate([x[:, :4] for x in (stats_o, stats_a, stats_b, stats_c)], axis=0)
    stats = stats.reshape(n_sec, 4 * row_dev)
    choose = (group[:, None] == s[None, :]).astype(jnp.float32)
    stats = jnp.dot(choose, stats, precision=lax.Precision.HIGHEST)
    send = jnp.broadcast_to(stats[:, None, :], (n_sec, n_ten, 4 * row_dev))
    send = send.reshape(n_sec * n_ten, 1, 4 * row_dev)
    got = lax.all_to_all(send, PLANE, 0, 0).reshape(n_sec * n_ten, row_dev, 4)

    tops = got[:, :, 0]
    top = jnp.max(tops, axis=0)
    scale = jnp.exp(tops - top[None])
    total = jnp.sum(got[:, :, 1] * scale, axis=0)
    moment = jnp.sum(got[:, :, 2] * scale, axis=0)
    picked = jnp.sum(got[:, :, 3], axis=0)
    lse = top + jnp.log(total)
    logp = picked - lse
    ent = lse - moment / total
    slot = jnp.arange(row_dev, dtype=jnp.int32)
    live = (slot < response_lengths[0]).astype(jnp.float32)
    return (logp * live, ent * live, (logp - ref_logp) * live)


def solution(mesh):
    tensor, dp = mesh.shape["tensor"], mesh.shape["dp"]
    mesh = Mesh(
        mesh.devices.reshape(2, NQ, NR, 2, tensor, dp), ("y_lo", "zq", "zr", "core", "tensor", "dp")
    )
    section = ("y_lo", "zq", "zr", "core")
    rows = P(section + ("dp",))
    in_specs = (P(section + ("dp",), "tensor"), P(None, section + ("tensor",)), rows, rows, rows)
    return jax.shard_map(
        per_device, mesh=mesh, in_specs=in_specs, out_specs=(rows, rows, rows), check_vma=False
    )
```

```python
import functools

import jax
import jax.numpy as jnp
from jax import lax
from jax.experimental import pallas as pl
from jax.experimental.pallas import tpu as pltpu
from jax.sharding import Mesh, PartitionSpec as P

NY, NZ, NR = 8, 12, 3
NQ = NZ // NR
LANES = 128
CHUNK = 1024
PLANE = ("y_lo", "zq", "zr", "core", "tensor")


def place(y, z, core):
    y, z = y % NY, z % NZ
    return ((y % 2) * NZ * 2 + z * 2 + core) * (NY // 2) + y // 2


def fetch(x, source):
    pairs = [
        (place(*source(y, z, c)), place(y, z, c))
        for y in range(NY)
        for z in range(NZ)
        for c in range(2)
    ]
    return lax.ppermute(x, PLANE, pairs)


def above(y, z, c):
    return y, z + 1, c


def below(y, z, c):
    return y, z - 1, c


def across(y, z, c):
    return y + 1 - 2 * c, z, c


def partner(y, z, c):
    return y, z, 1 - c


def stats_kernel(pieces, chunk, offset_ref, *refs):
    rows, (w_ref, out_ref, acc) = refs[:pieces], refs[pieces:]
    depth = w_ref.shape[0]
    for k in range(depth // chunk):
        x = jnp.concatenate([r[:, k * chunk : (k + 1) * chunk] for r in rows], axis=0)
        part = jnp.dot(x, w_ref[k * chunk : (k + 1) * chunk, :], preferred_element_type=jnp.float32)
        if k == 0:
            acc[...] = part
        else:
            acc[...] += part
    logits = acc[...]
    digits = jnp.concatenate([r[:, depth:] for r in rows], axis=0).astype(jnp.float32)
    ids = (digits[:, 2:3] * 256 + digits[:, 1:2]) * 256 + digits[:, 0:1]
    column = lax.broadcasted_iota(jnp.int32, logits.shape, 1) + offset_ref[0]
    top = jnp.max(logits, axis=1, keepdims=True)
    expo = jnp.exp(logits - top)
    total = jnp.sum(expo, axis=1, keepdims=True)
    moment = jnp.sum(expo * logits, axis=1, keepdims=True)
    hit = column == ids.astype(jnp.int32)
    picked = jnp.sum(jnp.where(hit, logits, 0.0), axis=1, keepdims=True)
    lane = lax.broadcasted_iota(jnp.int32, out_ref.shape, 1)
    low = jnp.where(lane == 0, top, total)
    high = jnp.where(lane == 2, moment, picked)
    out_ref[...] = jnp.where(lane < 2, low, high)


def stats_of(rows, weight, offset):
    count = sum(r.shape[0] for r in rows)
    depth, voc_dev = weight.shape
    return pl.pallas_call(
        functools.partial(stats_kernel, len(rows), CHUNK),
        out_shape=jax.ShapeDtypeStruct((count, LANES), jnp.float32),
        in_specs=[pl.BlockSpec(memory_space=pltpu.SMEM)]
        + [pl.BlockSpec(memory_space=pltpu.VMEM)] * (len(rows) + 1),
        out_specs=pl.BlockSpec(memory_space=pltpu.VMEM),
        scratch_shapes=[
            pltpu.VMEM((count, voc_dev), jnp.float32),
        ],
        compiler_params=pltpu.CompilerParams(vmem_limit_bytes=16 * 2**20),
        cost_estimate=pl.CostEstimate(
            flops=2 * count * depth * voc_dev,
            bytes_accessed=2 * depth * (count + voc_dev),
            transcendentals=count * voc_dev,
        ),
    )(offset, *rows, weight)


def per_device(hidden, vocab_weight, target_ids, ref_logp, response_lengths):
    row_dev, feat = hidden.shape
    voc_dev = vocab_weight.shape[1]
    y_lo, y_hi = lax.axis_index("y_lo"), lax.axis_index("tensor")
    core = lax.axis_index("core")
    z = lax.axis_index("zq") * NR + lax.axis_index("zr")
    section = (y_lo * NZ + z) * 2 + core
    n_sec, n_ten = 4 * NZ, NY // 2
    offset = ((section * n_ten + y_hi) * voc_dev).reshape(1).astype(jnp.int32)

    digits = jnp.stack([target_ids % 256, (target_ids // 256) % 256, target_ids // 65536], axis=1)
    digits = jnp.pad(digits.astype(jnp.bfloat16), ((0, 0), (0, LANES - 3)))
    block = jnp.concatenate([hidden, digits], axis=1)
    block = jnp.broadcast_to(block[None], (NQ * n_ten,) + block.shape)
    block = lax.all_to_all(block, ("zq", "tensor"), 0, 0)
    block = block.reshape(NQ, n_ten, row_dev, feat + LANES)
    pieces = [block[:, h, :, :feat] for h in range(n_ten)] + [block[:, 0, :, feat:]]
    unit = NQ * row_dev
    near = jnp.concatenate(pieces, axis=2).reshape(unit, n_ten * feat + LANES)

    up = fetch(near, above)
    down = fetch(near, below)
    side = fetch(near, across)
    side_up = jnp.where(core == 0, side, up)
    side_up = fetch(side_up, lambda y, z, c: (across if c else above)(y, z, c))
    side_down = jnp.where(core == 0, down, side)
    side_down = fetch(side_down, lambda y, z, c: (below if c else across)(y, z, c))
    early = jnp.concatenate([near, up, down, side], axis=0)
    early_p = fetch(early, partner)
    late = jnp.concatenate([side_up, side_down], axis=0)
    late_p = fetch(late, partner)
    stats_o = stats_of([near], vocab_weight, offset)
    stats_a = stats_of([up, down, side], vocab_weight, offset)
    stats_b = stats_of([early_p], vocab_weight, offset)
    stats_c = stats_of([late, late_p], vocab_weight, offset)

    s = jnp.arange(n_sec, dtype=jnp.int32)
    s_core, s_z, s_y = s % 2, (s // 2) % NZ, s // (2 * NZ)
    theirs = (s_core != core).astype(jnp.int32)
    unit = jnp.where(s_y == y_lo, 0, NR) + (s_z - z) % NR
    first = jnp.where(unit < 4, 4 * theirs + unit, 4 + 2 * theirs + unit)
    group = first * NQ + s_z // NR
    stats = jnp.concatenate([x[:, :4] for x in (stats_o, stats_a, stats_b, stats_c)], axis=0)
    stats = stats.reshape(n_sec, 4 * row_dev)
    choose = (jnp.repeat(group, n_ten)[:, None] == s[None, :]).astype(jnp.float32)
    send = jnp.dot(choose, stats, precision=lax.Precision.HIGHEST)[:, None, :]
    got = lax.all_to_all(send, PLANE, 0, 0).reshape(n_sec * n_ten, row_dev, 4)

    tops = got[:, :, 0]
    top = jnp.max(tops, axis=0)
    scale = jnp.exp(tops - top[None])
    total = jnp.sum(got[:, :, 1] * scale, axis=0)
    moment = jnp.sum(got[:, :, 2] * scale, axis=0)
    picked = jnp.sum(got[:, :, 3], axis=0)
    lse = top + jnp.log(total)
    logp = picked - lse
    ent = lse - moment / total
    slot = jnp.arange(row_dev, dtype=jnp.int32)
    live = (slot < response_lengths[0]).astype(jnp.float32)
    return (logp * live, ent * live, (logp - ref_logp) * live)


def solution(mesh):
    tensor, dp = mesh.shape["tensor"], mesh.shape["dp"]
    mesh = Mesh(
        mesh.devices.reshape(2, NQ, NR, 2, tensor, dp), ("y_lo", "zq", "zr", "core", "tensor", "dp")
    )
    section = ("y_lo", "zq", "zr", "core")
    rows = P(section + ("dp",))
    in_specs = (P(section + ("dp",), "tensor"), P(None, section + ("tensor",)), rows, rows, rows)
    return jax.shard_map(
        per_device, mesh=mesh, in_specs=in_specs, out_specs=(rows, rows, rows), check_vma=False
    )
```
